32 devices in a mesh: section: 4 (over y, x), replica: 8 (over z, core).
Axes of the slice: x: 2, y: 2, z: 4, core: 2. Of those that a mesh axis runs over, the one named last changes fastest.
Arguments:
- hidden: bfloat16 [4, 2048, 64], P('section', 'replica'), may hold values from -6 to 6
- out_grad: bfloat16 [4, 2048, 6144], P('section', 'replica'), may hold values from -6 to 6
- weights_old: bfloat16 [256, 6144], P('section'), may hold values from -6 to 6
- master: float32 [256, 6144], P(('section', 'replica')), may hold values from -6 to 6
- first_moment: float32 [256, 6144], P(('section', 'replica')), may hold values from -4 to 4
- second_moment: float32 [256, 6144], P(('section', 'replica')), may hold values from 0.01 to 1
- owner_order: int32 [8], replicated, may hold values from 0 to 7, each once
- step_count: int32 [1], replicated, may hold values from 1 to 8
Outputs:
- new_master: float32 [256, 6144], P(('section', 'replica'))
- new_first: float32 [256, 6144], P(('section', 'replica'))
- new_second: float32 [256, 6144], P(('section', 'replica'))
- checkpoint: float32 [3, 256, 6144], P(None, ('section', 'replica'))
- weights_new: bfloat16 [256, 6144], P('section')
- hidden_grad: bfloat16 [4, 2048, 64], P('section', 'replica')
The draws below stay inside these ranges and needn't reach their ends.
Inputs may be any that keep to these rules, and one draw needn't show every extreme that they name: Replica r owns block owner_order[r] of its section's bucket.
All inputs are finite; a program needn't handle non-finite values.
Results may differ from the reference program's by a relative error of at most 0.005.
Values may be sent and summed in bfloat16 or wider, within the bound.
No kernel may reach another device: no remote copies, remote signals or barrier semaphores. Data moves between devices by JAX's collectives and lax.ppermute only.
A program may use at most 64 MiB of HBM per device.

```python
import math
import jax
import jax.numpy as jnp
from jax import lax

D = 6144
SLAB_ROWS = 64
TOK_DEV = 256
TOKENS = 2048
SECTIONS = 4
N_SECTION = 4
N_REPLICA = 8


def strengthened(drawn, key, source, target, blocks, factor):
    def block_of(position):
        return (jnp.arange(drawn.shape[position]) // (drawn.shape[position] // blocks)).reshape((-1,) + (1,) * (drawn.ndim - 1 - position))

    near = jax.random.permutation(key, blocks)[block_of(target)]
    other_side = (block_of(target) + blocks // 2) % blocks
    return jnp.where((block_of(source) == near) | (block_of(source) == other_side), factor * drawn, drawn)


def shard_levels(own_key, shape, cuts, least, top_value):
    loudness = 1.0
    for axis_at, blocks in cuts:
        draws = jax.random.uniform(jax.random.fold_in(jax.random.fold_in(own_key, 6), axis_at), (blocks,), jnp.float32, least / len(cuts), top_value / len(cuts))
        loudness = loudness * jnp.repeat(jnp.exp(draws), shape[axis_at] // blocks).reshape((-1,) + (1,) * (len(shape) - 1 - axis_at))
    return loudness


def bell_draw(own_key, dims, width, bound, shards=(), kind=jnp.bfloat16):
    drawn = width * jax.random.normal(own_key, dims, jnp.float32)
    if shards:
        drawn = drawn * shard_levels(own_key, dims, shards, -0.22, 0.18)
    return jnp.clip(drawn, -bound, bound).astype(kind)


def noise_with(stream_key, shape, deviation, limit, shards, heavy, kind=jnp.bfloat16):
    array = deviation * jax.random.normal(stream_key, shape, jnp.float32)
    if shards:
        array = array * shard_levels(stream_key, shape, shards, -0.22, 0.18)
    return jnp.clip(strengthened(array, jax.random.fold_in(stream_key, 3), *heavy), -limit, limit).astype(kind)


def setup_inputs(seed: int = 0) -> dict:
    arg_keys = jax.random.split(jax.random.key(seed), 9)
    hidden = noise_with(arg_keys[0], (SECTIONS, TOKENS, SLAB_ROWS), 1.0, 6.0, ((0, 4), (1, 8)), (1, 2, 8, 2.0))
    out_grad = bell_draw(arg_keys[1], (SECTIONS, TOKENS, D), 1.0, 6.0, ((0, 4), (1, 8)))
    weights_old = bell_draw(arg_keys[2], (SECTIONS * SLAB_ROWS, D), 1.0, 6.0, ((0, 4),))
    master = bell_draw(arg_keys[3], (SECTIONS * SLAB_ROWS, D), 1.0, 6.0, ((0, 32),), jnp.float32)
    first_moment = bell_draw(arg_keys[4], (SECTIONS * SLAB_ROWS, D), 0.3, 4.0, ((0, 32),), jnp.float32)
    second_moment = jnp.clip(jnp.exp(math.log(1.0) - 4.6051702 * jax.random.uniform(arg_keys[5], (SECTIONS * SLAB_ROWS, D), jnp.float32) ** shard_levels(arg_keys[5], (SECTIONS * SLAB_ROWS, D), ((0, 32),), -0.2, 0.2)), 0.01, 1.0)
    owner_order = jax.random.permutation(arg_keys[6], N_REPLICA).astype(jnp.int32)
    step_count = jax.random.randint(arg_keys[7], (1,), 1, 9).astype(jnp.int32)
    return dict(hidden=hidden, out_grad=out_grad, weights_old=weights_old, master=master, first_moment=first_moment, second_moment=second_moment, owner_order=owner_order, step_count=step_count)


def adam_update(grads, master, first, second, steps):
    first_new = 0.9 * first + 0.1 * grads
    second_new = 0.95 * second + 0.05 * grads * grads
    fix_one = 1.0 - jnp.power(0.9, steps)
    fix_two = 1.0 - jnp.power(0.95, steps)
    update = first_new / fix_one / (jnp.sqrt(second_new / fix_two) + 1e-08)
    master_new = master - 0.05 * (update + 0.1 * master)
    return (master_new, first_new, second_new)

def reference(hidden, out_grad, weights_old, master, first_moment, second_moment, owner_order, step_count):
    factor = D ** (-0.5)
    block = SLAB_ROWS // N_REPLICA

    def per_section(operands):
        acts, grads_out, slab = operands
        slab_grad = lax.dot_general(acts, grads_out, (((0,), (0,)), ((), ())), preferred_element_type=jnp.float32) / TOK_DEV
        back = lax.dot_general(grads_out, slab, (((1,), (1,)), ((), ())), preferred_element_type=jnp.float32)
        return (slab_grad, (back * factor).astype(jnp.bfloat16))
    slab_grads, hidden_grad = lax.map(per_section, (hidden, out_grad, weights_old.reshape(N_SECTION, SLAB_ROWS, D)))
    owned = jnp.take(slab_grads.reshape(N_SECTION, N_REPLICA, block, D), owner_order, axis=1).reshape(N_SECTION * SLAB_ROWS, D)
    steps = step_count[0].astype(jnp.float32)
    new_master, new_first, new_second = adam_update(owned, master, first_moment, second_moment, steps)
    stacked = jnp.stack([new_master, new_first, new_second]).reshape(3, N_SECTION, N_REPLICA, block, D)
    checkpoint = jnp.roll(stacked, 1, axis=2).reshape(3, N_SECTION * SLAB_ROWS, D)
    inverse = jnp.zeros((N_REPLICA,), jnp.int32).at[owner_order].set(jnp.arange(N_REPLICA, dtype=jnp.int32))
    rounded = new_master.astype(jnp.bfloat16).reshape(N_SECTION, N_REPLICA, block, D)
    weights_new = jnp.take(rounded, inverse, axis=1).reshape(N_SECTION * SLAB_ROWS, D)
    return (new_master, new_first, new_second, checkpoint, weights_new, hidden_grad)
```

```python
import functools

import jax
import jax.numpy as jnp
from jax import lax
from jax.experimental import pallas as pl
from jax.experimental.pallas import tpu as pltpu
from jax.sharding import PartitionSpec as P


def passed_along(array, axis, by):
    devices = lax.axis_size(axis)
    return lax.ppermute(array, axis, [(i, (i + by) % devices) for i in range(devices)])


def adam_update(grads, master, first, second, fix_one, fix_two):
    first_new = 0.9 * first + 0.1 * grads
    second_new = 0.95 * second + 0.05 * grads * grads
    update = first_new / fix_one / (jnp.sqrt(second_new / fix_two) + 1e-08)
    master_new = master - 0.05 * (update + 0.1 * master)
    return (master_new, first_new, second_new)


def plain_device(
    hidden, out_grad, weights_old, master, first_moment, second_moment, owner_order, step_count
):
    replicas = lax.axis_size("replica")
    block = master.shape[0]
    slab_rows = weights_old.shape[0]
    width = out_grad.shape[2]
    acts = hidden[0]
    grads_out = out_grad[0]
    tokens = acts.shape[0]
    acts_blocks = acts.reshape(tokens, replicas, block)
    steps = step_count[0].astype(jnp.float32)
    columns = jnp.take(acts_blocks, owner_order, axis=1).reshape(tokens, slab_rows)
    product = lax.dot_general(
        columns, grads_out, (((0,), (0,)), ((), ())), preferred_element_type=jnp.float32
    )
    owned = lax.psum_scatter(product / tokens, "replica", scatter_dimension=0, tiled=True)
    back = lax.dot_general(
        grads_out, weights_old, (((1,), (1,)), ((), ())), preferred_element_type=jnp.float32
    )
    hidden_grad = (back * width ** (-0.5)).astype(jnp.bfloat16)
    fix_one = 1.0 - jnp.power(0.9, steps)
    fix_two = 1.0 - jnp.power(0.95, steps)
    updated = adam_update(owned, master, first_moment, second_moment, fix_one, fix_two)
    checkpoint = jnp.stack(passed_along(updated, "replica", 1))
    gathered = lax.all_gather(updated[0].astype(jnp.bfloat16), "replica", axis=0, tiled=True)
    inverse = (
        jnp.zeros((replicas,), jnp.int32).at[owner_order].set(jnp.arange(replicas, dtype=jnp.int32))
    )
    weights_new = jnp.take(gathered.reshape(replicas, block, width), inverse, axis=0).reshape(
        slab_rows, width
    )
    return (*updated, checkpoint, weights_new, hidden_grad[None])


SMEM = functools.partial(pl.BlockSpec, memory_space=pltpu.SMEM)
VMEM = functools.partial(pl.BlockSpec, memory_space=pltpu.VMEM)


def slab_kernel(
    steps, scale, order_hbm, acts_hbm, grads_hbm, send_ref, keep_ref, order, acts, grads, picked, sems
):
    replicas = order.shape[0]
    rows = acts.shape[0]
    block, half = rows // replicas, rows // 2
    tile = grads.shape[1] // steps
    small = [
        pltpu.make_async_copy(order_hbm, order, sems.at[steps]),
        pltpu.make_async_copy(acts_hbm, acts, sems.at[steps + 1]),
    ]
    spans = [pl.ds(step * tile, tile) for step in range(steps)]
    tiles = [
        pltpu.make_async_copy(grads_hbm.at[:, span], grads.at[:, span], sems.at[step])
        for step, span in enumerate(spans)
    ]
    for copy in small + tiles:
        copy.start()
    me = lax.axis_index("replica")
    chip, core = me // 2, me % 2
    at = lax.broadcasted_iota(jnp.int32, (rows, rows), 0)
    column = lax.broadcasted_iota(jnp.int32, (rows, rows), 1)
    source = at
    for copy in small:
        copy.wait()
    for place in range(replicas):
        away, mine = place % (replicas // 2), place // (replicas // 2)
        owner = 2 * (chip ^ away) + (core if mine else 1 - core)
        inside = (at >= place * block) & (at < (place + 1) * block)
        source = jnp.where(inside, at + (order[owner] - place) * block, source)
    chosen = jnp.where(column == source, 1.0, 0.0).astype(acts.dtype)
    picked[...] = jnp.dot(chosen, acts[...], preferred_element_type=jnp.float32).astype(
        picked.dtype
    )
    for copy, span in zip(tiles, spans):
        copy.wait()
        product = jnp.dot(picked[...], grads[:, span], preferred_element_type=jnp.float32) * scale
        send_ref[:, span] = product[:half].astype(send_ref.dtype)
        keep_ref[:, span] = product[half:]


def slab_product(order, acts_t, grads_out, steps):
    rows, tokens = acts_t.shape
    width = grads_out.shape[1]
    half = rows // 2
    return pl.pallas_call(
        functools.partial(slab_kernel, steps, 1.0 / tokens),
        in_specs=[pl.BlockSpec(memory_space=pltpu.HBM)] * 3,
        out_specs=[VMEM()] * 2,
        out_shape=[
            jax.ShapeDtypeStruct((half, width), jnp.bfloat16),
            jax.ShapeDtypeStruct((half, width), jnp.float32),
        ],
        scratch_shapes=[
            pltpu.SMEM(order.shape, order.dtype),
            pltpu.VMEM((rows, tokens), acts_t.dtype),
            pltpu.VMEM((tokens, width), grads_out.dtype),
            pltpu.VMEM((rows, tokens), acts_t.dtype),
            pltpu.SemaphoreType.DMA((steps + 2,)),
        ],
        compiler_params=pltpu.CompilerParams(vmem_limit_bytes=16 << 20),
        cost_estimate=pl.CostEstimate(
            flops=2 * rows * tokens * width,
            bytes_accessed=2 * tokens * width + 6 * half * width,
            transcendentals=0,
        ),
        name="slab_product",
    )(*(pltpu.with_memory_space_constraint(x, pltpu.HBM) for x in (order, acts_t, grads_out)))


def pair_kernel(keep_ref, got_ref, own_ref, *send_refs):
    block = own_ref.shape[0]
    own_ref[...] = keep_ref[:block] + got_ref[:block].astype(jnp.float32)
    for away, send in enumerate(send_refs, 1):
        rows = slice(away * block, (away + 1) * block)
        send[...] = (keep_ref[rows] + got_ref[rows].astype(jnp.float32)).astype(send.dtype)


def pair_sum(keep, got, block):
    rows, width = keep.shape
    others = rows // block - 1
    return pl.pallas_call(
        pair_kernel,
        in_specs=[VMEM(), VMEM()],
        out_specs=[VMEM()] * (1 + others),
        out_shape=[jax.ShapeDtypeStruct((block, width), jnp.float32)]
        + [jax.ShapeDtypeStruct((block, width), jnp.bfloat16)] * others,
        cost_estimate=pl.CostEstimate(
            flops=rows * width, bytes_accessed=8 * rows * width, transcendentals=0
        ),
        compiler_params=pltpu.CompilerParams(vmem_limit_bytes=8 << 20),
        name="pair_sum",
    )(keep, got)


def update_kernel(others, fix_ref, *refs):
    own, got, (master, first, second) = refs[0], refs[1 : 1 + others], refs[1 + others : 4 + others]
    new_master, new_first, new_second, send_master, send_first, send_second = refs[4 + others :]
    grads = own[...]
    for part in got:
        grads = grads + part[...].astype(jnp.float32)
    updated = adam_update(grads, master[...], first[...], second[...], fix_ref[0], fix_ref[1])
    new_master[...], new_first[...], new_second[...] = updated
    send_master[...] = updated[0].astype(send_master.dtype)
    send_first[...] = updated[1].astype(send_first.dtype)
    send_second[...] = updated[2].astype(send_second.dtype)


def update(fix, own, got, states, chunk, chunks):
    block, width = own.shape
    whole = pl.BlockSpec((block, width), lambda i: (0, 0))
    state = pl.BlockSpec((block, width), lambda i: (0, chunk))
    return pl.pallas_call(
        functools.partial(update_kernel, len(got)),
        grid=(1,),
        in_specs=[SMEM()] + [whole] * (1 + len(got)) + [state] * 3,
        out_specs=[whole] * 6,
        out_shape=[jax.ShapeDtypeStruct((block, width), jnp.float32)] * 3
        + [jax.ShapeDtypeStruct((block, width), jnp.bfloat16)] * 3,
        cost_estimate=pl.CostEstimate(
            flops=20 * block * width, bytes_accessed=40 * block * width, transcendentals=0
        ),
        compiler_params=pltpu.CompilerParams(vmem_limit_bytes=8 << 20),
        name="update",
    )(fix, own, *got, *states)


def placed_kernel(replicas, block, order_ref, *refs):
    pieces, (first, second) = refs[:replicas], refs[replicas : replicas + 2]
    weights, checkpoint = refs[replicas + 2 :]
    chips = replicas // 2
    me = lax.axis_index("replica")
    chip, core = me // 2, me % 2
    for place in range(replicas):
        away, other = place % chips, place // chips
        owner = 2 * (chip ^ away) + (1 - core if other else core)
        row = pl.multiple_of(order_ref[owner] * block, block)
        weights[pl.ds(row, block), :] = pieces[place][...]
        previous = lax.rem(me + replicas - 1, replicas)

        @pl.when(owner == previous)
        def _():
            checkpoint[0] = pieces[place][...].astype(jnp.float32)

    checkpoint[1] = first[...].astype(jnp.float32)
    checkpoint[2] = second[...].astype(jnp.float32)


def placed(order, pieces, first, second):
    block, width = first.shape
    replicas = order.shape[0]
    return pl.pallas_call(
        functools.partial(placed_kernel, replicas, block),
        in_specs=[SMEM()] + [VMEM()] * (replicas + 2),
        out_specs=[VMEM(), VMEM()],
        out_shape=[
            jax.ShapeDtypeStruct((replicas * block, width), jnp.bfloat16),
            jax.ShapeDtypeStruct((3, block, width), jnp.float32),
        ],
        compiler_params=pltpu.CompilerParams(vmem_limit_bytes=8 << 20),
        name="placed",
    )(order, *pieces, first, second)


def tiled_device(
    hidden, out_grad, weights_old, master, first_moment, second_moment, owner_order, step_count
):
    replicas = lax.axis_size("replica")
    chips = replicas // 2
    block = master.shape[0]
    width = out_grad.shape[2]
    grads_out = out_grad[0]
    acts_t = hidden[0].T
    sibling = [(i, i ^ 1) for i in range(replicas)]
    across = {k: [(i, i ^ (2 * k)) for i in range(replicas)] for k in range(1, chips)}
    ring = [(i, (i + 1) % replicas) for i in range(replicas)]
    steps = step_count[0].astype(jnp.float32)
    fix = jnp.stack([1.0 - jnp.power(0.9, steps), 1.0 - jnp.power(0.95, steps)])

    send, keep = slab_product(owner_order, acts_t, grads_out, 4)
    got = lax.ppermute(send, "replica", sibling)
    own, *sends = pair_sum(keep, got, block)
    arrived = [lax.ppermute(s, "replica", across[k]) for k, s in enumerate(sends, 1)]
    late_weights, late_grads, _ = lax.optimization_barrier((weights_old, grads_out, own))
    back = lax.dot_general(
        late_weights, late_grads, (((1,), (1,)), ((), ())), preferred_element_type=jnp.float32
    )
    hidden_grad = (back * width ** (-0.5)).astype(jnp.bfloat16).T
    fix, hidden_grad = lax.optimization_barrier((fix, hidden_grad))
    *updated, send_master, send_first, send_second = update(
        fix, own, arrived, (master, first_moment, second_moment), 0, 1
    )
    near = [send_master] + [
        lax.ppermute(send_master, "replica", across[k]) for k in range(1, chips)
    ]
    moved_first = lax.ppermute(send_first, "replica", ring)
    moved_second = lax.ppermute(send_second, "replica", ring)
    far = [lax.ppermute(piece, "replica", sibling) for piece in near]
    weights_new, checkpoint = placed(owner_order, near + far, moved_first, moved_second)
    return (*updated, checkpoint, weights_new, hidden_grad[None])


def per_device(*arrays):
    replicas = lax.axis_size("replica")
    chips = replicas // 2
    block, width = arrays[3].shape
    fits = block % 8 == 0 and width % 512 == 0 and replicas % 2 == 0 and chips & (chips - 1) == 0
    return (tiled_device if fits else plain_device)(*arrays)


def solution(mesh):
    placed_specs = (
        P("section", "replica", None),
        P("section", "replica", None),
        P("section", None),
        P(("section", "replica"), None),
        P(("section", "replica"), None),
        P(("section", "replica"), None),
        P(),
        P(),
    )
    return jax.shard_map(
        per_device,
        mesh=mesh,
        in_specs=placed_specs,
        out_specs=(
            P(("section", "replica"), None),
            P(("section", "replica"), None),
            P(("section", "replica"), None),
            P(None, ("section", "replica"), None),
            P("section", None),
            P("section", "replica", None),
        ),
        check_vma=False,
    )
```

```python
import functools

import jax
import jax.numpy as jnp
from jax import lax
from jax.experimental import pallas as pl
from jax.experimental.pallas import tpu as pltpu
from jax.sharding import PartitionSpec as P


def passed_along(array, axis, by):
    devices = lax.axis_size(axis)
    return lax.ppermute(array, axis, [(i, (i + by) % devices) for i in range(devices)])


def adam_update(grads, master, first, second, fix_one, fix_two):
    first_new = 0.9 * first + 0.1 * grads
    second_new = 0.95 * second + 0.05 * grads * grads
    update = first_new / fix_one / (jnp.sqrt(second_new / fix_two) + 1e-08)
    master_new = master - 0.05 * (update + 0.1 * master)
    return (master_new, first_new, second_new)


def plain_device(
    hidden, out_grad, weights_old, master, first_moment, second_moment, owner_order, step_count
):
    replicas = lax.axis_size("replica")
    block = master.shape[0]
    slab_rows = weights_old.shape[0]
    width = out_grad.shape[2]
    acts = hidden[0]
    grads_out = out_grad[0]
    tokens = acts.shape[0]
    acts_blocks = acts.reshape(tokens, replicas, block)
    steps = step_count[0].astype(jnp.float32)
    columns = jnp.take(acts_blocks, owner_order, axis=1).reshape(tokens, slab_rows)
    product = lax.dot_general(
        columns, grads_out, (((0,), (0,)), ((), ())), preferred_element_type=jnp.float32
    )
    owned = lax.psum_scatter(product / tokens, "replica", scatter_dimension=0, tiled=True)
    back = lax.dot_general(
        grads_out, weights_old, (((1,), (1,)), ((), ())), preferred_element_type=jnp.float32
    )
    hidden_grad = (back * width ** (-0.5)).astype(jnp.bfloat16)
    fix_one = 1.0 - jnp.power(0.9, steps)
    fix_two = 1.0 - jnp.power(0.95, steps)
    updated = adam_update(owned, master, first_moment, second_moment, fix_one, fix_two)
    checkpoint = jnp.stack(passed_along(updated, "replica", 1))
    gathered = lax.all_gather(updated[0].astype(jnp.bfloat16), "replica", axis=0, tiled=True)
    inverse = (
        jnp.zeros((replicas,), jnp.int32).at[owner_order].set(jnp.arange(replicas, dtype=jnp.int32))
    )
    weights_new = jnp.take(gathered.reshape(replicas, block, width), inverse, axis=0).reshape(
        slab_rows, width
    )
    return (*updated, checkpoint, weights_new, hidden_grad[None])


SMEM = functools.partial(pl.BlockSpec, memory_space=pltpu.SMEM)
VMEM = functools.partial(pl.BlockSpec, memory_space=pltpu.VMEM)
HBM = functools.partial(pl.BlockSpec, memory_space=pltpu.HBM)


def params():
    return pltpu.CompilerParams(vmem_limit_bytes=8 << 20)


def cost(flops, moved):
    return pl.CostEstimate(flops=flops, bytes_accessed=moved, transcendentals=0)


def in_hbm(*arrays):
    return tuple(pltpu.with_memory_space_constraint(x, pltpu.HBM) for x in arrays)


def this_core():
    return lax.axis_index("replica") % 2


def distances_of(chips, core):
    ks = sorted(range(1, chips), key=lambda k: (k ^ (chips >> 1), k))
    return [0] + (ks[-1:] + ks[:-1] if core else ks)


def distance_at(place, chips, core):
    first, second = (distances_of(chips, c)[place] for c in range(2))
    return jnp.where(core == 0, first, second)


def send_kernel(
    order_hbm, acts_hbm, grads_hbm, first_hbm, second_hbm,
    send_ref, grads, picked, first, second, moments, order, acts, sems,
):
    replicas = order.shape[0]
    rows, tokens = acts.shape
    block, half = rows // replicas, rows // 2
    steps = sems.shape[0] - 4
    tile = grads.shape[1] // steps
    small = [
        pltpu.make_async_copy(order_hbm, order, sems.at[steps]),
        pltpu.make_async_copy(acts_hbm, acts, sems.at[steps + 1]),
    ]
    spans = [pl.ds(step * tile, tile) for step in range(steps)]
    tiles = [
        pltpu.make_async_copy(grads_hbm.at[:, span], grads.at[:, span], sems.at[step])
        for step, span in enumerate(spans)
    ]
    states = [
        pltpu.make_async_copy(first_hbm, first, sems.at[steps + 2]),
        pltpu.make_async_copy(second_hbm, second, sems.at[steps + 3]),
    ]
    for copy in small + tiles + states:
        copy.start()
    me = lax.axis_index("replica")
    chip, core = me // 2, me % 2
    at = lax.broadcasted_iota(jnp.int32, (rows, rows), 0)
    column = lax.broadcasted_iota(jnp.int32, (rows, rows), 1)
    source = at
    for copy in small:
        copy.wait()
    for place in range(replicas):
        at_place, mine = place % (replicas // 2), place // (replicas // 2)
        lane = core if mine else 1 - core
        owner = 2 * (chip ^ distance_at(at_place, replicas // 2, lane)) + lane
        inside = (at >= place * block) & (at < (place + 1) * block)
        source = jnp.where(inside, at + (order[owner] - place) * block, source)
    chosen = jnp.where(column == source, 1.0, 0.0).astype(acts.dtype)
    both = jnp.dot(chosen, acts[...], preferred_element_type=jnp.float32).astype(picked.dtype)
    picked[...] = both[half:]
    mine = both[:half]
    for copy, span in zip(tiles, spans):
        copy.wait()
        product = jnp.dot(mine, grads[:, span], preferred_element_type=jnp.float32)
        send_ref[:, span] = (product * (1.0 / tokens)).astype(send_ref.dtype)
    for at, (copy, state) in enumerate(zip(states, (first, second))):
        copy.wait()
        moments[at * block : (at + 1) * block] = state[...].astype(moments.dtype)


def slab_to_send(order, acts_t, grads_out, first, second, steps):
    rows, tokens = acts_t.shape
    block = first.shape[0]
    width = grads_out.shape[1]
    return pl.pallas_call(
        send_kernel,
        in_specs=[HBM()] * 5,
        out_specs=[VMEM()] * 6,
        out_shape=[
            jax.ShapeDtypeStruct((rows // 2, width), jnp.bfloat16),
            jax.ShapeDtypeStruct((tokens, width), grads_out.dtype),
            jax.ShapeDtypeStruct((rows // 2, tokens), acts_t.dtype),
            jax.ShapeDtypeStruct((block, width), jnp.float32),
            jax.ShapeDtypeStruct((block, width), jnp.float32),
            jax.ShapeDtypeStruct((2 * block, width), jnp.bfloat16),
        ],
        scratch_shapes=[
            pltpu.SMEM(order.shape, order.dtype),
            pltpu.VMEM((rows, tokens), acts_t.dtype),
            pltpu.SemaphoreType.DMA((steps + 4,)),
        ],
        compiler_params=params(),
        cost_estimate=cost(rows * tokens * width, 2 * tokens * width),
        name="slab_to_send",
    )(*in_hbm(order, acts_t, grads_out, first, second))


def keep_kernel(picked, grads, master_hbm, keep_ref, master, sem):
    copy = pltpu.make_async_copy(master_hbm, master, sem)
    copy.start()
    tokens = grads.shape[0]
    tile = grads.shape[1] // 4
    for step in range(4):
        span = pl.ds(step * tile, tile)
        product = jnp.dot(picked[...], grads[:, span], preferred_element_type=jnp.float32)
        keep_ref[:, span] = product * (1.0 / tokens)
    copy.wait()


def slab_to_keep(picked, grads, master):
    rows, tokens = picked.shape
    width = master.shape[1]
    return pl.pallas_call(
        keep_kernel,
        in_specs=[VMEM()] * 2 + [HBM()],
        out_specs=[VMEM()] * 2,
        out_shape=[
            jax.ShapeDtypeStruct((rows, width), jnp.float32),
            jax.ShapeDtypeStruct(master.shape, jnp.float32),
        ],
        scratch_shapes=[pltpu.SemaphoreType.DMA],
        compiler_params=params(),
        cost_estimate=cost(2 * rows * tokens * width, 2 * tokens * width),
        name="slab_to_keep",
    )(picked, grads, *in_hbm(master))


def back_kernel(scale, core, weights_hbm, grads, *refs):
    out, weights, result, sems, sem = refs[-5:]
    steps = sems.shape[0]
    tile = grads.shape[1] // steps

    @pl.when(this_core() == core)
    def _():
        spans = [pl.ds(step * tile, tile) for step in range(steps)]
        copies = [
            pltpu.make_async_copy(weights_hbm.at[:, span], weights.at[:, span], sems.at[step])
            for step, span in enumerate(spans)
        ]
        for copy in copies:
            copy.start()
        total = None
        for copy, span in zip(copies, spans):
            copy.wait()
            term = lax.dot_general(
                weights[:, span], grads[:, span], (((1,), (1,)), ((), ())),
                preferred_element_type=jnp.float32,
            )
            total = term if total is None else total + term
        result[...] = (total * scale).astype(result.dtype)
        copy = pltpu.make_async_copy(result, out, sem)
        copy.start()
        copy.wait()


def hidden_gradient(weights_old, grads, core, steps, earlier=()):
    rows, width = weights_old.shape
    tokens = grads.shape[0]
    return pl.pallas_call(
        functools.partial(back_kernel, width ** (-0.5), core),
        in_specs=[HBM(), VMEM()] + [HBM()] * len(earlier),
        out_specs=HBM(),
        out_shape=jax.ShapeDtypeStruct((rows, tokens), jnp.bfloat16),
        input_output_aliases={2 + at: at for at in range(len(earlier))},
        scratch_shapes=[
            pltpu.VMEM((rows, width), weights_old.dtype),
            pltpu.VMEM((rows, tokens), jnp.bfloat16),
            pltpu.SemaphoreType.DMA((steps,)),
            pltpu.SemaphoreType.DMA,
        ],
        compiler_params=params(),
        cost_estimate=cost(2 * rows * tokens * width, 2 * (tokens + rows) * width),
        name="hidden_gradient",
    )(*in_hbm(weights_old), grads, *earlier)


def pair_kernel(keep_ref, got_ref, own_ref, *send_refs):
    block = own_ref.shape[0]
    own_ref[...] = keep_ref[:block] + got_ref[:block].astype(jnp.float32)
    for away, send in enumerate(send_refs, 1):
        rows = slice(away * block, (away + 1) * block)
        send[...] = (keep_ref[rows] + got_ref[rows].astype(jnp.float32)).astype(send.dtype)


def pair_sum(keep, got, block):
    rows, width = keep.shape
    others = rows // block - 1
    return pl.pallas_call(
        pair_kernel,
        in_specs=[VMEM(), VMEM()],
        out_specs=[VMEM()] * (1 + others),
        out_shape=[jax.ShapeDtypeStruct((block, width), jnp.float32)]
        + [jax.ShapeDtypeStruct((block, width), jnp.bfloat16)] * others,
        compiler_params=params(),
        cost_estimate=cost(rows * width, 8 * rows * width),
        name="pair_sum",
    )(keep, got)


def update_kernel(fix_ref, *refs):
    parts, (master, first, second, grads_ref, send_master, send_grads) = refs[:-6], refs[-6:]
    grads = parts[0][...]
    for part in parts[1:]:
        grads = grads + part[...].astype(jnp.float32)
    grads_ref[...] = grads
    send_grads[...] = grads.astype(send_grads.dtype)
    new_master, _, _ = adam_update(
        grads, master[...], first[...], second[...], fix_ref[0:1, 0:1], fix_ref[1:2, 0:1]
    )
    send_master[...] = new_master.astype(send_master.dtype)


def update(fix, parts, states):
    block, width = parts[0].shape
    return pl.pallas_call(
        update_kernel,
        in_specs=[VMEM()] * (4 + len(parts)),
        out_specs=[VMEM()] * 3,
        out_shape=[
            jax.ShapeDtypeStruct((block, width), jnp.float32),
            jax.ShapeDtypeStruct((block, width), jnp.bfloat16),
            jax.ShapeDtypeStruct((block, width), jnp.bfloat16),
        ],
        compiler_params=params(),
        cost_estimate=cost(20 * block * width, 24 * block * width),
        name="update",
    )(fix, *parts, *states)


def states_kernel(fix_ref, master, first, second, grads, *outs):
    updated = adam_update(
        grads[...], master[...], first[...], second[...], fix_ref[0:1, 0:1], fix_ref[1:2, 0:1]
    )
    for out, value in zip(outs, updated):
        out[...] = value


def new_states(fix, states, grads):
    shape = states[0].shape
    return pl.pallas_call(
        states_kernel,
        in_specs=[VMEM()] * 5,
        out_specs=[VMEM()] * 3,
        out_shape=[jax.ShapeDtypeStruct(shape, jnp.float32)] * 3,
        compiler_params=params(),
        cost_estimate=cost(20 * states[0].size, 28 * states[0].size),
        name="new_states",
    )(fix, *states, grads)


def owner_at(place, chips, sibling):
    me = lax.axis_index("replica")
    lane = 1 - me % 2 if sibling else me % 2
    return 2 * (me // 2 ^ distance_at(place, chips, lane)) + lane


def place_kernel(chips, order, *refs):
    near, far = refs[:chips], refs[chips : 2 * chips]
    packed, moved, weights, checkpoint, partner, sems = refs[2 * chips :]
    block = moved.shape[0]
    replicas = order.shape[0]
    previous = lax.rem(lax.axis_index("replica") + replicas - 1, replicas)
    copies = []
    for sibling, pieces in enumerate((near, far)):
        for at, piece in enumerate(pieces):
            row = pl.multiple_of(order[owner_at(at, chips, sibling)] * block, block)
            target = weights.at[pl.ds(row, block), :]
            copies.append(pltpu.make_async_copy(piece, target, sems.at[len(copies)]))
    for copy in copies:
        copy.start()
    grads = moved[...].astype(jnp.float32)
    partner[1] = 0.9 * packed[:block].astype(jnp.float32) + 0.1 * grads
    partner[2] = 0.95 * packed[block:].astype(jnp.float32) + 0.05 * grads * grads
    for at, piece in enumerate(far):

        @pl.when(owner_at(at, chips, 1) == previous)
        def _():
            partner[0] = piece[...].astype(jnp.float32)

    last = pltpu.make_async_copy(partner, checkpoint, sems.at[replicas])
    last.start()
    for copy in copies:
        copy.wait()
    last.wait()


def place(order, near, far, packed, moved):
    block, width = moved.shape
    chips = len(near)
    rows = 2 * chips * block
    return pl.pallas_call(
        functools.partial(place_kernel, chips),
        in_specs=[SMEM()] + [VMEM()] * (2 * chips + 2),
        out_specs=[HBM()] * 2,
        out_shape=[
            jax.ShapeDtypeStruct((rows, width), jnp.bfloat16),
            jax.ShapeDtypeStruct((3, block, width), jnp.float32),
        ],
        scratch_shapes=[
            pltpu.VMEM((3, block, width), jnp.float32),
            pltpu.SemaphoreType.DMA((2 * chips + 1,)),
        ],
        compiler_params=params(),
        cost_estimate=cost(0, 8 * rows * width),
        name="place",
    )(order, *near, *far, packed, moved)


def tiled_device(
    hidden, out_grad, weights_old, master, first_moment, second_moment, owner_order, step_count
):
    replicas = lax.axis_size("replica")
    chips = replicas // 2
    block, _ = master.shape

    def permuted(piece, target):
        return lax.ppermute(piece, "replica", [(i, target(i)) for i in range(replicas)])

    def across(piece, at):
        ks = [distances_of(chips, core)[at] for core in range(2)]
        return permuted(piece, lambda i: i ^ (2 * ks[i % 2]))

    def to_sibling(piece):
        return permuted(piece, lambda i: i ^ 1)

    def along_ring(piece):
        return permuted(piece, lambda i: (i + 1) % replicas)

    steps = step_count[0].astype(jnp.float32)
    fix = jnp.stack([1.0 - jnp.power(0.9, steps), 1.0 - jnp.power(0.95, steps)])
    fix = jnp.broadcast_to(fix[:, None], (2, 128))

    send, grads_out, picked, first, second, packed = slab_to_send(
        owner_order, hidden[0].T, out_grad[0], first_moment, second_moment, 4
    )
    got = to_sibling(send)
    keep, loaded = slab_to_keep(picked, grads_out, master)
    states = (loaded, first, second)
    packed = along_ring(packed)
    own, *sends = pair_sum(keep, got, block)
    hidden_grad = hidden_gradient(weights_old, grads_out, 1, 2)
    hidden_grad = hidden_gradient(weights_old, grads_out, 0, 2, (hidden_grad,))
    parts = [own] + [across(sends[k - 1], k) for k in range(1, chips)]
    grads, send_master, send_grads = update(fix, parts, states)
    near = [send_master] + [across(send_master, k) for k in range(1, chips)]
    updated = new_states(fix, states, grads)
    moved = along_ring(send_grads)
    far = [to_sibling(piece) for piece in near]
    weights_new, checkpoint = place(owner_order, near, far, packed, moved)
    return (*updated, checkpoint, weights_new, hidden_grad.T[None])


def fits(replicas, block, width):
    chips = replicas // 2
    return block % 8 == 0 and width % 512 == 0 and replicas % 2 == 0 and chips & (chips - 1) == 0


def per_device(*arrays):
    block, width = arrays[3].shape
    if not fits(lax.axis_size("replica"), block, width):
        return plain_device(*arrays)
    return tiled_device(*arrays)


def solution(mesh):
    devices = P(("section", "replica"), None)
    return jax.shard_map(
        per_device,
        mesh=mesh,
        in_specs=(
            P("section", "replica", None),
            P("section", "replica", None),
            P("section", None),
            devices,
            devices,
            devices,
            P(),
            P(),
        ),
        out_specs=(
            devices,
            devices,
            devices,
            P(None, ("section", "replica"), None),
            P("section", None),
            P("section", "replica", None),
        ),
        check_vma=False,
    )
```

```python
import functools
import math

import jax
import jax.numpy as jnp
from jax import lax
from jax.experimental import pallas as pl
from jax.experimental.pallas import tpu as pltpu
from jax.sharding import PartitionSpec as P


def passed_along(array, axis, by):
    devices = lax.axis_size(axis)
    return lax.ppermute(array, axis, [(i, (i + by) % devices) for i in range(devices)])


def adam_update(grads, master, first, second, fix_one, fix_two):
    first_new = 0.9 * first + 0.1 * grads
    second_new = 0.95 * second + 0.05 * grads * grads
    update = first_new / fix_one / (jnp.sqrt(second_new / fix_two) + 1e-08)
    master_new = master - 0.05 * (update + 0.1 * master)
    return (master_new, first_new, second_new)


def plain_device(
    hidden, out_grad, weights_old, master, first_moment, second_moment, owner_order, step_count
):
    replicas = lax.axis_size("replica")
    block = master.shape[0]
    slab_rows = weights_old.shape[0]
    width = out_grad.shape[2]
    acts = hidden[0]
    grads_out = out_grad[0]
    tokens = acts.shape[0]
    acts_blocks = acts.reshape(tokens, replicas, block)
    steps = step_count[0].astype(jnp.float32)
    columns = jnp.take(acts_blocks, owner_order, axis=1).reshape(tokens, slab_rows)
    product = lax.dot_general(
        columns, grads_out, (((0,), (0,)), ((), ())), preferred_element_type=jnp.float32
    )
    owned = lax.psum_scatter(product / tokens, "replica", scatter_dimension=0, tiled=True)
    back = lax.dot_general(
        grads_out, weights_old, (((1,), (1,)), ((), ())), preferred_element_type=jnp.float32
    )
    hidden_grad = (back * width ** (-0.5)).astype(jnp.bfloat16)
    fix_one = 1.0 - jnp.power(0.9, steps)
    fix_two = 1.0 - jnp.power(0.95, steps)
    updated = adam_update(owned, master, first_moment, second_moment, fix_one, fix_two)
    checkpoint = jnp.stack(passed_along(updated, "replica", 1))
    gathered = lax.all_gather(updated[0].astype(jnp.bfloat16), "replica", axis=0, tiled=True)
    inverse = (
        jnp.zeros((replicas,), jnp.int32).at[owner_order].set(jnp.arange(replicas, dtype=jnp.int32))
    )
    weights_new = jnp.take(gathered.reshape(replicas, block, width), inverse, axis=0).reshape(
        slab_rows, width
    )
    return (*updated, checkpoint, weights_new, hidden_grad[None])


SMEM = functools.partial(pl.BlockSpec, memory_space=pltpu.SMEM)
VMEM = functools.partial(pl.BlockSpec, memory_space=pltpu.VMEM)
HBM = functools.partial(pl.BlockSpec, memory_space=pltpu.HBM)


def params():
    return pltpu.CompilerParams(vmem_limit_bytes=8 << 20)


def cost(flops, moved):
    return pl.CostEstimate(flops=flops, bytes_accessed=moved, transcendentals=0)


def in_hbm(*arrays):
    return tuple(pltpu.with_memory_space_constraint(x, pltpu.HBM) for x in arrays)


def this_core():
    return lax.axis_index("replica") % 2


SUM_MOVES = ((("xor", 2), ("xor", 1), ("xor", 3)), (("xor", 1), ("xor", 2), ("xor", 3)))
GATHER_MOVES = ((("xor", 2), ("xor", 1), ("xor", 3)), (("xor", 2), ("xor", 1), ("xor", 3)))


def move_of(moves, chips, core, place):
    if place == 0:
        return ("on", 0)
    return moves[core][place - 1] if len(moves[core]) == chips - 1 else ("on", place)


def moved_chip(chip, chips, move, back=False):
    kind, by = move
    if kind == "xor":
        return chip ^ by
    by = chips - by if back else by
    return lax.rem(chip + by, chips) if isinstance(chip, jax.Array) else (chip + by) % chips


def owner_at(place, chips, core, moves, back):
    chip = lax.axis_index("replica") // 2
    first, second = (
        2 * moved_chip(chip, chips, move_of(moves, chips, c, place), back) + c for c in range(2)
    )
    return jnp.where(core == 0, first, second)


def send_kernel(
    order_hbm, acts_hbm, grads_hbm, first_hbm, second_hbm,
    send_ref, grads, picked, first, second, moments, table, order, acts, sems,
):
    replicas = order.shape[0]
    rows, tokens = acts.shape
    block, half = rows // replicas, rows // 2
    steps = sems.shape[0] - 4
    tile = grads.shape[1] // steps
    small = [
        pltpu.make_async_copy(order_hbm, order, sems.at[steps]),
        pltpu.make_async_copy(acts_hbm, acts, sems.at[steps + 1]),
    ]
    spans = [pl.ds(step * tile, tile) for step in range(steps)]
    tiles = [
        pltpu.make_async_copy(grads_hbm.at[:, span], grads.at[:, span], sems.at[step])
        for step, span in enumerate(spans)
    ]
    states = [
        pltpu.make_async_copy(first_hbm, first, sems.at[steps + 2]),
        pltpu.make_async_copy(second_hbm, second, sems.at[steps + 3]),
    ]
    for copy in small + tiles + states:
        copy.start()
    core = this_core()
    at = lax.broadcasted_iota(jnp.int32, (rows, rows), 0)
    column = lax.broadcasted_iota(jnp.int32, (rows, rows), 1)
    source = at
    for copy in small:
        copy.wait()
    for place in range(replicas):
        at_place, mine = place % (replicas // 2), place // (replicas // 2)
        lane = core if mine else 1 - core
        owner = owner_at(at_place, replicas // 2, lane, SUM_MOVES, False)
        inside = (at >= place * block) & (at < (place + 1) * block)
        source = jnp.where(inside, at + (order[owner] - place) * block, source)
    chosen = jnp.where(column == source, 1.0, 0.0).astype(acts.dtype)
    both = jnp.dot(chosen, acts[...], preferred_element_type=jnp.float32).astype(picked.dtype)
    picked[...] = both[half:]
    line = lax.broadcasted_iota(jnp.int32, table.shape, 0)
    value = jnp.zeros(table.shape, jnp.int32)
    for place in range(replicas):
        at_place, far = place % (replicas // 2), place // (replicas // 2)
        owner = owner_at(at_place, replicas // 2, 1 - core if far else core, GATHER_MOVES, True)
        value = jnp.where(line == place, order[owner] * block, value)
    table[...] = value
    mine = both[:half]
    for copy, span in zip(tiles, spans):
        copy.wait()
        product = jnp.dot(mine, grads[:, span], preferred_element_type=jnp.float32)
        send_ref[:, span] = (product * (1.0 / tokens)).astype(send_ref.dtype)
    for at, (copy, state) in enumerate(zip(states, (first, second))):
        copy.wait()
        moments[at * block : (at + 1) * block] = state[...].astype(moments.dtype)


def slab_to_send(order, acts_t, grads_out, first, second, steps):
    rows, tokens = acts_t.shape
    block = first.shape[0]
    width = grads_out.shape[1]
    return pl.pallas_call(
        send_kernel,
        in_specs=[HBM()] * 5,
        out_specs=[VMEM()] * 7,
        out_shape=[
            jax.ShapeDtypeStruct((rows // 2, width), jnp.bfloat16),
            jax.ShapeDtypeStruct((tokens, width), grads_out.dtype),
            jax.ShapeDtypeStruct((rows // 2, tokens), acts_t.dtype),
            jax.ShapeDtypeStruct((block, width), jnp.float32),
            jax.ShapeDtypeStruct((block, width), jnp.float32),
            jax.ShapeDtypeStruct((2 * block, width), jnp.bfloat16),
            jax.ShapeDtypeStruct((order.shape[0], 128), jnp.int32),
        ],
        scratch_shapes=[
            pltpu.SMEM(order.shape, order.dtype),
            pltpu.VMEM((rows, tokens), acts_t.dtype),
            pltpu.SemaphoreType.DMA((steps + 4,)),
        ],
        compiler_params=params(),
        cost_estimate=cost(rows * tokens * width, 2 * tokens * width),
        name="slab_to_send",
    )(*in_hbm(order, acts_t, grads_out, first, second))


def keep_kernel(picked, grads, master_hbm, keep_ref, master, sem):
    copy = pltpu.make_async_copy(master_hbm, master, sem)
    copy.start()
    tokens = grads.shape[0]
    tile = grads.shape[1] // 4
    for step in range(4):
        span = pl.ds(step * tile, tile)
        product = jnp.dot(picked[...], grads[:, span], preferred_element_type=jnp.float32)
        keep_ref[:, span] = product * (1.0 / tokens)
    copy.wait()


def slab_to_keep(picked, grads, master):
    rows, tokens = picked.shape
    width = master.shape[1]
    return pl.pallas_call(
        keep_kernel,
        in_specs=[VMEM()] * 2 + [HBM()],
        out_specs=[VMEM()] * 2,
        out_shape=[
            jax.ShapeDtypeStruct((rows, width), jnp.float32),
            jax.ShapeDtypeStruct(master.shape, jnp.float32),
        ],
        scratch_shapes=[pltpu.SemaphoreType.DMA],
        compiler_params=params(),
        cost_estimate=cost(2 * rows * tokens * width, 2 * tokens * width),
        name="slab_to_keep",
    )(picked, grads, *in_hbm(master))


def back_kernel(scale, core, weights_hbm, grads, *refs):
    out, weights, result, sems, sem = refs[-5:]
    steps = sems.shape[0]
    tile = grads.shape[1] // steps

    @pl.when(this_core() == core)
    def _():
        spans = [pl.ds(step * tile, tile) for step in range(steps)]
        copies = [
            pltpu.make_async_copy(weights_hbm.at[:, span], weights.at[:, span], sems.at[step])
            for step, span in enumerate(spans)
        ]
        for copy in copies:
            copy.start()
        total = None
        for copy, span in zip(copies, spans):
            copy.wait()
            term = lax.dot_general(
                weights[:, span], grads[:, span], (((1,), (1,)), ((), ())),
                preferred_element_type=jnp.float32,
            )
            total = term if total is None else total + term
        result[...] = (total * scale).astype(result.dtype)
        copy = pltpu.make_async_copy(result, out, sem)
        copy.start()
        copy.wait()


def hidden_gradient(weights_old, grads, core, steps, earlier=()):
    rows, width = weights_old.shape
    tokens = grads.shape[0]
    return pl.pallas_call(
        functools.partial(back_kernel, width ** (-0.5), core),
        in_specs=[HBM(), VMEM()] + [HBM()] * len(earlier),
        out_specs=HBM(),
        out_shape=jax.ShapeDtypeStruct((rows, tokens), jnp.bfloat16),
        input_output_aliases={2 + at: at for at in range(len(earlier))},
        scratch_shapes=[
            pltpu.VMEM((rows, width), weights_old.dtype),
            pltpu.VMEM((rows, tokens), jnp.bfloat16),
            pltpu.SemaphoreType.DMA((steps,)),
            pltpu.SemaphoreType.DMA,
        ],
        compiler_params=params(),
        cost_estimate=cost(2 * rows * tokens * width, 2 * (tokens + rows) * width),
        name="hidden_gradient",
    )(*in_hbm(weights_old), grads, *earlier)


def pair_kernel(keep_ref, got_ref, own_ref, *send_refs):
    block = own_ref.shape[0]
    own_ref[...] = keep_ref[:block] + got_ref[:block].astype(jnp.float32)
    for away, send in enumerate(send_refs, 1):
        rows = slice(away * block, (away + 1) * block)
        send[...] = (keep_ref[rows] + got_ref[rows].astype(jnp.float32)).astype(send.dtype)


def pair_sum(keep, got, block):
    rows, width = keep.shape
    others = rows // block - 1
    return pl.pallas_call(
        pair_kernel,
        in_specs=[VMEM(), VMEM()],
        out_specs=[VMEM()] * (1 + others),
        out_shape=[jax.ShapeDtypeStruct((block, width), jnp.float32)]
        + [jax.ShapeDtypeStruct((block, width), jnp.bfloat16)] * others,
        compiler_params=params(),
        cost_estimate=cost(rows * width, 8 * rows * width),
        name="pair_sum",
    )(keep, got)


def rates_kernel(count, out):
    line = lax.broadcasted_iota(jnp.int32, out.shape, 0)
    log = jnp.where(line < out.shape[0] // 2, math.log(0.9), math.log(0.95))
    out[...] = 1.0 - jnp.exp(count[0].astype(jnp.float32) * log)


def corrections(count):
    return pl.pallas_call(
        rates_kernel,
        in_specs=[SMEM()],
        out_specs=VMEM(),
        out_shape=jax.ShapeDtypeStruct((16, 128), jnp.float32),
        compiler_params=params(),
        cost_estimate=cost(0, 8192),
        name="corrections",
    )(count)


def update_kernel(fix, *refs):
    parts, (master, first, second, grads_ref, send_master, send_grads) = refs[:-6], refs[-6:]
    grads = parts[0][...]
    for part in parts[1:]:
        grads = grads + part[...].astype(jnp.float32)
    grads_ref[...] = grads
    send_grads[...] = grads.astype(send_grads.dtype)
    new_master, _, _ = adam_update(
        grads, master[...], first[...], second[...], fix[0:1, 0:1], fix[8:9, 0:1]
    )
    send_master[...] = new_master.astype(send_master.dtype)


def update(fix, parts, states):
    block, width = parts[0].shape
    return pl.pallas_call(
        update_kernel,
        in_specs=[VMEM()] * (4 + len(parts)),
        out_specs=[VMEM()] * 3,
        out_shape=[
            jax.ShapeDtypeStruct((block, width), jnp.float32),
            jax.ShapeDtypeStruct((block, width), jnp.bfloat16),
            jax.ShapeDtypeStruct((block, width), jnp.bfloat16),
        ],
        compiler_params=params(),
        cost_estimate=cost(20 * block * width, 24 * block * width),
        name="update",
    )(fix, *parts, *states)


def states_kernel(fix, master, first, second, grads, *outs):
    updated = adam_update(
        grads[...], master[...], first[...], second[...], fix[0:1, 0:1], fix[8:9, 0:1]
    )
    for out, value in zip(outs, updated):
        out[...] = value


def new_states(fix, states, grads):
    shape = states[0].shape
    return pl.pallas_call(
        states_kernel,
        in_specs=[VMEM()] * 5,
        out_specs=[VMEM()] * 3,
        out_shape=[jax.ShapeDtypeStruct(shape, jnp.float32)] * 3,
        compiler_params=params(),
        cost_estimate=cost(20 * states[0].size, 28 * states[0].size),
        name="new_states",
    )(fix, *states, grads)


def place_kernel(chips, table, *refs):
    near, far = refs[:chips], refs[chips : 2 * chips]
    packed, moved, weights, checkpoint, partner, sems = refs[2 * chips :]
    block = moved.shape[0]
    replicas = 2 * chips
    me = lax.axis_index("replica")
    previous = lax.rem(me + replicas - 1, replicas)
    rows = table[...]
    copies = []
    for at, piece in enumerate((*near, *far)):
        target = weights.at[pl.ds(pl.multiple_of(rows[at, 0], block), block), :]
        copies.append(pltpu.make_async_copy(piece, target, sems.at[at]))
    for copy in copies:
        copy.start()
    grads = moved[...].astype(jnp.float32)
    partner[1] = 0.9 * packed[:block].astype(jnp.float32) + 0.1 * grads
    partner[2] = 0.95 * packed[block:].astype(jnp.float32) + 0.05 * grads * grads
    for at, piece in enumerate(far):

        @pl.when(owner_at(at, chips, 1 - me % 2, GATHER_MOVES, True) == previous)
        def _():
            partner[0] = piece[...].astype(jnp.float32)

    last = pltpu.make_async_copy(partner, checkpoint, sems.at[replicas])
    last.start()
    for copy in copies:
        copy.wait()
    last.wait()


def place(table, near, far, packed, moved):
    block, width = moved.shape
    chips = len(near)
    rows = 2 * chips * block
    return pl.pallas_call(
        functools.partial(place_kernel, chips),
        in_specs=[VMEM()] * (2 * chips + 3),
        out_specs=[HBM()] * 2,
        out_shape=[
            jax.ShapeDtypeStruct((rows, width), jnp.bfloat16),
            jax.ShapeDtypeStruct((3, block, width), jnp.float32),
        ],
        scratch_shapes=[
            pltpu.VMEM((3, block, width), jnp.float32),
            pltpu.SemaphoreType.DMA((2 * chips + 1,)),
        ],
        compiler_params=params(),
        cost_estimate=cost(0, 8 * rows * width),
        name="place",
    )(table, *near, *far, packed, moved)


def tiled_device(
    hidden, out_grad, weights_old, master, first_moment, second_moment, owner_order, step_count
):
    replicas = lax.axis_size("replica")
    chips = replicas // 2
    block, _ = master.shape

    def permuted(piece, target):
        return lax.ppermute(piece, "replica", [(i, target(i)) for i in range(replicas)])

    def across(piece, at, moves):
        def target(i):
            return 2 * moved_chip(i // 2, chips, move_of(moves, chips, i % 2, at)) + i % 2

        return permuted(piece, target)

    def to_sibling(piece):
        return permuted(piece, lambda i: i ^ 1)

    def along_ring(piece):
        return permuted(piece, lambda i: (i + 1) % replicas)

    send, grads_out, picked, first, second, packed, table = slab_to_send(
        owner_order, hidden[0].T, out_grad[0], first_moment, second_moment, 4
    )
    got = to_sibling(send)
    keep, loaded = slab_to_keep(picked, grads_out, master)
    states = (loaded, first, second)
    packed = along_ring(packed)
    own, *sends = pair_sum(keep, got, block)
    hidden_grad = hidden_gradient(weights_old, grads_out, 1, 2)
    hidden_grad = hidden_gradient(weights_old, grads_out, 0, 2, (hidden_grad,))
    parts = [own] + [across(sends[k - 1], k, SUM_MOVES) for k in range(1, chips)]
    fix = corrections(lax.optimization_barrier((step_count, own))[0])
    grads, send_master, send_grads = update(fix, parts, states)
    near = [send_master] + [across(send_master, k, GATHER_MOVES) for k in range(1, chips)]
    updated = new_states(fix, states, grads)
    moved = along_ring(send_grads)
    far = [to_sibling(piece) for piece in near]
    weights_new, checkpoint = place(table, near, far, packed, moved)
    return (*updated, checkpoint, weights_new, hidden_grad.T[None])


def fits(replicas, block, width):
    chips = replicas // 2
    return block % 8 == 0 and width % 512 == 0 and replicas % 2 == 0 and chips & (chips - 1) == 0


def per_device(*arrays):
    block, width = arrays[3].shape
    if not fits(lax.axis_size("replica"), block, width):
        return plain_device(*arrays)
    return tiled_device(*arrays)


def solution(mesh):
    devices = P(("section", "replica"), None)
    return jax.shard_map(
        per_device,
        mesh=mesh,
        in_specs=(
            P("section", "replica", None),
            P("section", "replica", None),
            P("section", None),
            devices,
            devices,
            devices,
            P(),
            P(),
        ),
        out_specs=(
            devices,
            devices,
            devices,
            P(None, ("section", "replica"), None),
            P("section", None),
            P("section", "replica", None),
        ),
        check_vma=False,
    )
```

```python
import functools
import math

import jax
import jax.numpy as jnp
from jax import lax
from jax.experimental import pallas as pl
from jax.experimental.pallas import tpu as pltpu
from jax.sharding import PartitionSpec as P


def passed_along(array, axis, by):
    devices = lax.axis_size(axis)
    return lax.ppermute(array, axis, [(i, (i + by) % devices) for i in range(devices)])


def adam_update(grads, master, first, second, fix_one, fix_two):
    first_new = 0.9 * first + 0.1 * grads
    second_new = 0.95 * second + 0.05 * grads * grads
    update = first_new / fix_one / (jnp.sqrt(second_new / fix_two) + 1e-08)
    master_new = master - 0.05 * (update + 0.1 * master)
    return (master_new, first_new, second_new)


def plain_device(
    hidden, out_grad, weights_old, master, first_moment, second_moment, owner_order, step_count
):
    replicas = lax.axis_size("replica")
    block = master.shape[0]
    slab_rows = weights_old.shape[0]
    width = out_grad.shape[2]
    acts = hidden[0]
    grads_out = out_grad[0]
    tokens = acts.shape[0]
    acts_blocks = acts.reshape(tokens, replicas, block)
    steps = step_count[0].astype(jnp.float32)
    columns = jnp.take(acts_blocks, owner_order, axis=1).reshape(tokens, slab_rows)
    product = lax.dot_general(
        columns, grads_out, (((0,), (0,)), ((), ())), preferred_element_type=jnp.float32
    )
    owned = lax.psum_scatter(product / tokens, "replica", scatter_dimension=0, tiled=True)
    back = lax.dot_general(
        grads_out, weights_old, (((1,), (1,)), ((), ())), preferred_element_type=jnp.float32
    )
    hidden_grad = (back * width ** (-0.5)).astype(jnp.bfloat16)
    fix_one = 1.0 - jnp.power(0.9, steps)
    fix_two = 1.0 - jnp.power(0.95, steps)
    updated = adam_update(owned, master, first_moment, second_moment, fix_one, fix_two)
    checkpoint = jnp.stack(passed_along(updated, "replica", 1))
    gathered = lax.all_gather(updated[0].astype(jnp.bfloat16), "replica", axis=0, tiled=True)
    inverse = (
        jnp.zeros((replicas,), jnp.int32).at[owner_order].set(jnp.arange(replicas, dtype=jnp.int32))
    )
    weights_new = jnp.take(gathered.reshape(replicas, block, width), inverse, axis=0).reshape(
        slab_rows, width
    )
    return (*updated, checkpoint, weights_new, hidden_grad[None])


SMEM = functools.partial(pl.BlockSpec, memory_space=pltpu.SMEM)
VMEM = functools.partial(pl.BlockSpec, memory_space=pltpu.VMEM)
HBM = functools.partial(pl.BlockSpec, memory_space=pltpu.HBM)


def params():
    return pltpu.CompilerParams(vmem_limit_bytes=8 << 20)


def cost(flops, moved):
    return pl.CostEstimate(flops=flops, bytes_accessed=moved, transcendentals=0)


def in_hbm(*arrays):
    return tuple(pltpu.with_memory_space_constraint(x, pltpu.HBM) for x in arrays)


def this_core():
    return lax.axis_index("replica") % 2


SUM_MOVES = ((("xor", 2), ("xor", 1), ("xor", 3)), (("xor", 1), ("xor", 2), ("xor", 3)))
GATHER_MOVES = ((("xor", 2), ("xor", 1), ("xor", 3)), (("xor", 2), ("xor", 1), ("xor", 3)))


def move_of(moves, chips, core, place):
    if place == 0:
        return ("on", 0)
    return moves[core][place - 1] if len(moves[core]) == chips - 1 else ("on", place)


def moved_chip(chip, chips, move, back=False):
    kind, by = move
    if kind == "xor":
        return chip ^ by
    by = chips - by if back else by
    return lax.rem(chip + by, chips) if isinstance(chip, jax.Array) else (chip + by) % chips


def owner_at(place, chips, core, moves, back):
    chip = lax.axis_index("replica") // 2
    first, second = (
        2 * moved_chip(chip, chips, move_of(moves, chips, c, place), back) + c for c in range(2)
    )
    return jnp.where(core == 0, first, second)


def send_kernel(
    order_hbm, acts_hbm, grads_hbm, first_hbm, second_hbm,
    send_ref, grads, picked, first, second, moments, table, order, acts, sems,
):
    replicas = order.shape[0]
    rows, tokens = acts.shape
    block, half = rows // replicas, rows // 2
    steps = sems.shape[0] - 4
    tile = grads.shape[1] // steps
    small = [
        pltpu.make_async_copy(order_hbm, order, sems.at[steps]),
        pltpu.make_async_copy(acts_hbm, acts, sems.at[steps + 1]),
    ]
    spans = [pl.ds(step * tile, tile) for step in range(steps)]
    tiles = [
        pltpu.make_async_copy(grads_hbm.at[:, span], grads.at[:, span], sems.at[step])
        for step, span in enumerate(spans)
    ]
    states = [
        pltpu.make_async_copy(first_hbm, first, sems.at[steps + 2]),
        pltpu.make_async_copy(second_hbm, second, sems.at[steps + 3]),
    ]
    for copy in small + tiles + states:
        copy.start()
    core = this_core()
    at = lax.broadcasted_iota(jnp.int32, (rows, rows), 0)
    column = lax.broadcasted_iota(jnp.int32, (rows, rows), 1)
    source = at
    for copy in small:
        copy.wait()
    for place in range(replicas):
        at_place, mine = place % (replicas // 2), place // (replicas // 2)
        lane = core if mine else 1 - core
        owner = owner_at(at_place, replicas // 2, lane, SUM_MOVES, False)
        inside = (at >= place * block) & (at < (place + 1) * block)
        source = jnp.where(inside, at + (order[owner] - place) * block, source)
    chosen = jnp.where(column == source, 1.0, 0.0).astype(acts.dtype)
    both = jnp.dot(chosen, acts[...], preferred_element_type=jnp.float32).astype(picked.dtype)
    picked[...] = both[half:]
    line = lax.broadcasted_iota(jnp.int32, table.shape, 0)
    value = jnp.zeros(table.shape, jnp.int32)
    for place in range(replicas):
        at_place, far = place % (replicas // 2), place // (replicas // 2)
        owner = owner_at(at_place, replicas // 2, 1 - core if far else core, GATHER_MOVES, True)
        value = jnp.where(line == place, order[owner] * block, value)
    table[...] = value
    mine = both[:half]
    for copy, span in zip(tiles, spans):
        copy.wait()
        product = jnp.dot(mine, grads[:, span], preferred_element_type=jnp.float32)
        send_ref[:, span] = (product * (1.0 / tokens)).astype(send_ref.dtype)
    for at, (copy, state) in enumerate(zip(states, (first, second))):
        copy.wait()
        moments[at * block : (at + 1) * block] = state[...].astype(moments.dtype)


def slab_to_send(order, acts_t, grads_out, first, second, steps):
    rows, tokens = acts_t.shape
    block = first.shape[0]
    width = grads_out.shape[1]
    return pl.pallas_call(
        send_kernel,
        in_specs=[HBM()] * 5,
        out_specs=[VMEM()] * 7,
        out_shape=[
            jax.ShapeDtypeStruct((rows // 2, width), jnp.bfloat16),
            jax.ShapeDtypeStruct((tokens, width), grads_out.dtype),
            jax.ShapeDtypeStruct((rows // 2, tokens), acts_t.dtype),
            jax.ShapeDtypeStruct((block, width), jnp.float32),
            jax.ShapeDtypeStruct((block, width), jnp.float32),
            jax.ShapeDtypeStruct((2 * block, width), jnp.bfloat16),
            jax.ShapeDtypeStruct((order.shape[0], 128), jnp.int32),
        ],
        scratch_shapes=[
            pltpu.SMEM(order.shape, order.dtype),
            pltpu.VMEM((rows, tokens), acts_t.dtype),
            pltpu.SemaphoreType.DMA((steps + 4,)),
        ],
        compiler_params=params(),
        cost_estimate=cost(rows * tokens * width, 2 * tokens * width),
        name="slab_to_send",
    )(*in_hbm(order, acts_t, grads_out, first, second))


def keep_kernel(picked, grads, master_hbm, keep_ref, master, sem):
    copy = pltpu.make_async_copy(master_hbm, master, sem)
    copy.start()
    tokens = grads.shape[0]
    tile = grads.shape[1] // 4
    for step in range(4):
        span = pl.ds(step * tile, tile)
        product = jnp.dot(picked[...], grads[:, span], preferred_element_type=jnp.float32)
        keep_ref[:, span] = product * (1.0 / tokens)
    copy.wait()


def slab_to_keep(picked, grads, master):
    rows, tokens = picked.shape
    width = master.shape[1]
    return pl.pallas_call(
        keep_kernel,
        in_specs=[VMEM()] * 2 + [HBM()],
        out_specs=[VMEM()] * 2,
        out_shape=[
            jax.ShapeDtypeStruct((rows, width), jnp.float32),
            jax.ShapeDtypeStruct(master.shape, jnp.float32),
        ],
        scratch_shapes=[pltpu.SemaphoreType.DMA],
        compiler_params=params(),
        cost_estimate=cost(2 * rows * tokens * width, 2 * tokens * width),
        name="slab_to_keep",
    )(picked, grads, *in_hbm(master))


def back_kernel(scale, core, weights_hbm, grads, *refs):
    out, weights, result, sems, sem = refs[-5:]
    steps = sems.shape[0]
    tile = grads.shape[1] // steps

    @pl.when(this_core() == core)
    def _():
        spans = [pl.ds(step * tile, tile) for step in range(steps)]
        copies = [
            pltpu.make_async_copy(weights_hbm.at[:, span], weights.at[:, span], sems.at[step])
            for step, span in enumerate(spans)
        ]
        for copy in copies:
            copy.start()
        total = None
        for copy, span in zip(copies, spans):
            copy.wait()
            term = lax.dot_general(
                weights[:, span], grads[:, span], (((1,), (1,)), ((), ())),
                preferred_element_type=jnp.float32,
            )
            total = term if total is None else total + term
        result[...] = (total * scale).astype(result.dtype)
        copy = pltpu.make_async_copy(result, out, sem)
        copy.start()
        copy.wait()


def hidden_gradient(weights_old, grads, core, steps, earlier=()):
    rows, width = weights_old.shape
    tokens = grads.shape[0]
    return pl.pallas_call(
        functools.partial(back_kernel, width ** (-0.5), core),
        in_specs=[HBM(), VMEM()] + [HBM()] * len(earlier),
        out_specs=HBM(),
        out_shape=jax.ShapeDtypeStruct((rows, tokens), jnp.bfloat16),
        input_output_aliases={2 + at: at for at in range(len(earlier))},
        scratch_shapes=[
            pltpu.VMEM((rows, width), weights_old.dtype),
            pltpu.VMEM((rows, tokens), jnp.bfloat16),
            pltpu.SemaphoreType.DMA((steps,)),
            pltpu.SemaphoreType.DMA,
        ],
        compiler_params=params(),
        cost_estimate=cost(2 * rows * tokens * width, 2 * (tokens + rows) * width),
        name="hidden_gradient",
    )(*in_hbm(weights_old), grads, *earlier)


def pair_kernel(keep_ref, got_ref, own_ref, *send_refs):
    block = own_ref.shape[0]
    own_ref[...] = keep_ref[:block] + got_ref[:block].astype(jnp.float32)
    for away, send in enumerate(send_refs, 1):
        rows = slice(away * block, (away + 1) * block)
        send[...] = (keep_ref[rows] + got_ref[rows].astype(jnp.float32)).astype(send.dtype)


def pair_sum(keep, got, block):
    rows, width = keep.shape
    others = rows // block - 1
    return pl.pallas_call(
        pair_kernel,
        in_specs=[VMEM(), VMEM()],
        out_specs=[VMEM()] * (1 + others),
        out_shape=[jax.ShapeDtypeStruct((block, width), jnp.float32)]
        + [jax.ShapeDtypeStruct((block, width), jnp.bfloat16)] * others,
        compiler_params=params(),
        cost_estimate=cost(rows * width, 8 * rows * width),
        name="pair_sum",
    )(keep, got)


def rates_kernel(count, out):
    line = lax.broadcasted_iota(jnp.int32, out.shape, 0)
    log = jnp.where(line < out.shape[0] // 2, math.log(0.9), math.log(0.95))
    out[...] = 1.0 - jnp.exp(count[0].astype(jnp.float32) * log)


def corrections(count):
    return pl.pallas_call(
        rates_kernel,
        in_specs=[SMEM()],
        out_specs=VMEM(),
        out_shape=jax.ShapeDtypeStruct((16, 128), jnp.float32),
        compiler_params=params(),
        cost_estimate=cost(0, 8192),
        name="corrections",
    )(count)


def update_kernel(fix, *refs):
    parts, (master, first, second, grads_ref, send_master, send_grads) = refs[:-6], refs[-6:]
    grads = parts[0][...]
    for part in parts[1:]:
        grads = grads + part[...].astype(jnp.float32)
    grads_ref[...] = grads
    send_grads[...] = grads.astype(send_grads.dtype)
    new_master, _, _ = adam_update(
        grads, master[...], first[...], second[...], fix[0:1, 0:1], fix[8:9, 0:1]
    )
    send_master[...] = new_master.astype(send_master.dtype)


def update(fix, parts, states):
    block, width = parts[0].shape
    return pl.pallas_call(
        update_kernel,
        in_specs=[VMEM()] * (4 + len(parts)),
        out_specs=[VMEM()] * 3,
        out_shape=[
            jax.ShapeDtypeStruct((block, width), jnp.float32),
            jax.ShapeDtypeStruct((block, width), jnp.bfloat16),
            jax.ShapeDtypeStruct((block, width), jnp.bfloat16),
        ],
        compiler_params=params(),
        cost_estimate=cost(20 * block * width, 24 * block * width),
        name="update",
    )(fix, *parts, *states)


def states_kernel(fix, master, first, second, grads, *outs):
    updated = adam_update(
        grads[...], master[...], first[...], second[...], fix[0:1, 0:1], fix[8:9, 0:1]
    )
    for out, value in zip(outs, updated):
        out[...] = value


def new_states(fix, states, grads):
    shape = states[0].shape
    return pl.pallas_call(
        states_kernel,
        in_specs=[VMEM()] * 5,
        out_specs=[VMEM()] * 3,
        out_shape=[jax.ShapeDtypeStruct(shape, jnp.float32)] * 3,
        compiler_params=params(),
        cost_estimate=cost(20 * states[0].size, 28 * states[0].size),
        name="new_states",
    )(fix, *states, grads)


def placing(places, chips, table, near, far, weights, sems):
    block = near[0].shape[0]
    rows = table[...]
    copies = []
    for at, *pieces in zip(places, near, far):
        for sibling, piece in enumerate(pieces):
            row = pl.multiple_of(rows[at + sibling * chips, 0], block)
            target = weights.at[pl.ds(row, block), :]
            copies.append(pltpu.make_async_copy(piece, target, sems.at[len(copies)]))
    return copies


def early_kernel(chips, table, *refs):
    count = chips - 1
    copies = placing(range(count), chips, table, refs[:count], refs[count : 2 * count], *refs[-2:])
    for copy in copies:
        copy.start()
    for copy in copies:
        copy.wait()


def place_early(table, near, far):
    block, width = near[0].shape
    chips = len(near) + 1
    return pl.pallas_call(
        functools.partial(early_kernel, chips),
        in_specs=[VMEM()] * (2 * chips - 1),
        out_specs=HBM(),
        out_shape=jax.ShapeDtypeStruct((2 * chips * block, width), jnp.bfloat16),
        scratch_shapes=[pltpu.SemaphoreType.DMA((2 * chips - 2,))],
        compiler_params=params(),
        cost_estimate=cost(0, 8 * chips * block * width),
        name="place_early",
    )(table, *near, *far)


def late_kernel(chips, table, near, *refs):
    far, (packed, moved, _, weights, checkpoint, partner, sems) = refs[:chips], refs[chips:]
    block = moved.shape[0]
    replicas = 2 * chips
    me = lax.axis_index("replica")
    previous = lax.rem(me + replicas - 1, replicas)
    copies = placing([chips - 1], chips, table, [near], far[-1:], weights, sems)
    for copy in copies:
        copy.start()
    grads = moved[...].astype(jnp.float32)
    partner[1] = 0.9 * packed[:block].astype(jnp.float32) + 0.1 * grads
    partner[2] = 0.95 * packed[block:].astype(jnp.float32) + 0.05 * grads * grads
    for at, piece in enumerate(far):

        @pl.when(owner_at(at, chips, 1 - me % 2, GATHER_MOVES, True) == previous)
        def _():
            partner[0] = piece[...].astype(jnp.float32)

    last = pltpu.make_async_copy(partner, checkpoint, sems.at[2])
    last.start()
    for copy in copies:
        copy.wait()
    last.wait()


def place_late(table, near, far, packed, moved, weights):
    block, width = moved.shape
    chips = len(far)
    return pl.pallas_call(
        functools.partial(late_kernel, chips),
        in_specs=[VMEM()] * (chips + 4) + [HBM()],
        out_specs=[HBM()] * 2,
        out_shape=[
            jax.ShapeDtypeStruct(weights.shape, weights.dtype),
            jax.ShapeDtypeStruct((3, block, width), jnp.float32),
        ],
        input_output_aliases={chips + 4: 0},
        scratch_shapes=[
            pltpu.VMEM((3, block, width), jnp.float32),
            pltpu.SemaphoreType.DMA((3,)),
        ],
        compiler_params=params(),
        cost_estimate=cost(0, 20 * block * width),
        name="place_late",
    )(table, near, *far, packed, moved, weights)


def tiled_device(
    hidden, out_grad, weights_old, master, first_moment, second_moment, owner_order, step_count
):
    replicas = lax.axis_size("replica")
    chips = replicas // 2
    block, _ = master.shape

    def permuted(piece, target):
        return lax.ppermute(piece, "replica", [(i, target(i)) for i in range(replicas)])

    def across(piece, at, moves):
        def target(i):
            return 2 * moved_chip(i // 2, chips, move_of(moves, chips, i % 2, at)) + i % 2

        return permuted(piece, target)

    def to_sibling(piece):
        return permuted(piece, lambda i: i ^ 1)

    def along_ring(piece):
        return permuted(piece, lambda i: (i + 1) % replicas)

    send, grads_out, picked, first, second, packed, table = slab_to_send(
        owner_order, hidden[0].T, out_grad[0], first_moment, second_moment, 4
    )
    got = to_sibling(send)
    keep, loaded = slab_to_keep(picked, grads_out, master)
    states = (loaded, first, second)
    packed = along_ring(packed)
    own, *sends = pair_sum(keep, got, block)
    hidden_grad = hidden_gradient(weights_old, grads_out, 1, 2)
    hidden_grad = hidden_gradient(weights_old, grads_out, 0, 2, (hidden_grad,))
    parts = [own] + [across(sends[k - 1], k, SUM_MOVES) for k in range(1, chips)]
    fix = corrections(lax.optimization_barrier((step_count, own))[0])
    grads, send_master, send_grads = update(fix, parts, states)
    near = [send_master] + [across(send_master, k, GATHER_MOVES) for k in range(1, chips)]
    updated = new_states(fix, states, grads)
    moved = along_ring(send_grads)
    far = [to_sibling(piece) for piece in near]
    weights_new = place_early(table, near[:-1], far[:-1])
    weights_new, checkpoint = place_late(table, near[-1], far, packed, moved, weights_new)
    return (*updated, checkpoint, weights_new, hidden_grad.T[None])


def fits(replicas, block, width):
    chips = replicas // 2
    return block % 8 == 0 and width % 512 == 0 and replicas % 2 == 0 and chips & (chips - 1) == 0


def per_device(*arrays):
    block, width = arrays[3].shape
    if not fits(lax.axis_size("replica"), block, width):
        return plain_device(*arrays)
    return tiled_device(*arrays)


def solution(mesh):
    devices = P(("section", "replica"), None)
    return jax.shard_map(
        per_device,
        mesh=mesh,
        in_specs=(
            P("section", "replica", None),
            P("section", "replica", None),
            P("section", None),
            devices,
            devices,
            devices,
            P(),
            P(),
        ),
        out_specs=(
            devices,
            devices,
            devices,
            P(None, ("section", "replica"), None),
            P("section", None),
            P("section", "replica", None),
        ),
        check_vma=False,
    )
```

```python
import functools
import math

import jax
import jax.numpy as jnp
from jax import lax
from jax.experimental import pallas as pl
from jax.experimental.pallas import tpu as pltpu
from jax.sharding import PartitionSpec as P


def passed_along(array, axis, by):
    devices = lax.axis_size(axis)
    return lax.ppermute(array, axis, [(i, (i + by) % devices) for i in range(devices)])


def adam_update(grads, master, first, second, fix_one, fix_two):
    first_new = 0.9 * first + 0.1 * grads
    second_new = 0.95 * second + 0.05 * grads * grads
    update = first_new / fix_one / (jnp.sqrt(second_new / fix_two) + 1e-08)
    master_new = master - 0.05 * (update + 0.1 * master)
    return (master_new, first_new, second_new)


def plain_device(
    hidden, out_grad, weights_old, master, first_moment, second_moment, owner_order, step_count
):
    replicas = lax.axis_size("replica")
    block = master.shape[0]
    slab_rows = weights_old.shape[0]
    width = out_grad.shape[2]
    acts = hidden[0]
    grads_out = out_grad[0]
    tokens = acts.shape[0]
    acts_blocks = acts.reshape(tokens, replicas, block)
    steps = step_count[0].astype(jnp.float32)
    columns = jnp.take(acts_blocks, owner_order, axis=1).reshape(tokens, slab_rows)
    product = lax.dot_general(
        columns, grads_out, (((0,), (0,)), ((), ())), preferred_element_type=jnp.float32
    )
    owned = lax.psum_scatter(product / tokens, "replica", scatter_dimension=0, tiled=True)
    back = lax.dot_general(
        grads_out, weights_old, (((1,), (1,)), ((), ())), preferred_element_type=jnp.float32
    )
    hidden_grad = (back * width ** (-0.5)).astype(jnp.bfloat16)
    fix_one = 1.0 - jnp.power(0.9, steps)
    fix_two = 1.0 - jnp.power(0.95, steps)
    updated = adam_update(owned, master, first_moment, second_moment, fix_one, fix_two)
    checkpoint = jnp.stack(passed_along(updated, "replica", 1))
    gathered = lax.all_gather(updated[0].astype(jnp.bfloat16), "replica", axis=0, tiled=True)
    inverse = (
        jnp.zeros((replicas,), jnp.int32).at[owner_order].set(jnp.arange(replicas, dtype=jnp.int32))
    )
    weights_new = jnp.take(gathered.reshape(replicas, block, width), inverse, axis=0).reshape(
        slab_rows, width
    )
    return (*updated, checkpoint, weights_new, hidden_grad[None])


SMEM = functools.partial(pl.BlockSpec, memory_space=pltpu.SMEM)
VMEM = functools.partial(pl.BlockSpec, memory_space=pltpu.VMEM)
HBM = functools.partial(pl.BlockSpec, memory_space=pltpu.HBM)


def params():
    return pltpu.CompilerParams(vmem_limit_bytes=8 << 20)


def cost(flops, moved):
    return pl.CostEstimate(flops=flops, bytes_accessed=moved, transcendentals=0)


def in_hbm(*arrays):
    return tuple(pltpu.with_memory_space_constraint(x, pltpu.HBM) for x in arrays)


def this_core():
    return lax.axis_index("replica") % 2


SUM_MOVES = ((("xor", 2), ("xor", 1), ("xor", 3)), (("xor", 1), ("xor", 2), ("xor", 3)))
GATHER_MOVES = ((("xor", 2), ("xor", 1), ("xor", 3)), (("xor", 2), ("xor", 1), ("xor", 3)))


def move_of(moves, chips, core, place):
    if place == 0:
        return ("on", 0)
    return moves[core][place - 1] if len(moves[core]) == chips - 1 else ("on", place)


def moved_chip(chip, chips, move, back=False):
    kind, by = move
    if kind == "xor":
        return chip ^ by
    by = chips - by if back else by
    return lax.rem(chip + by, chips) if isinstance(chip, jax.Array) else (chip + by) % chips


def owner_at(place, chips, core, moves, back):
    chip = lax.axis_index("replica") // 2
    first, second = (
        2 * moved_chip(chip, chips, move_of(moves, chips, c, place), back) + c for c in range(2)
    )
    return jnp.where(core == 0, first, second)


def place_of_row(row):
    return 1 - row if row < 2 else row


def send_kernel(
    order_hbm, acts_hbm, grads_hbm, first_hbm, second_hbm,
    first_send, other_send, grads, picked, first, second, moments, table, order, acts, sems,
):
    replicas = order.shape[0]
    rows, tokens = acts.shape
    block, half = rows // replicas, rows // 2
    steps = sems.shape[0] - 4
    tile = grads.shape[1] // steps
    small = [
        pltpu.make_async_copy(order_hbm, order, sems.at[steps]),
        pltpu.make_async_copy(acts_hbm, acts, sems.at[steps + 1]),
    ]
    spans = [pl.ds(step * tile, tile) for step in range(steps)]
    tiles = [
        pltpu.make_async_copy(grads_hbm.at[:, span], grads.at[:, span], sems.at[step])
        for step, span in enumerate(spans)
    ]
    states = [
        pltpu.make_async_copy(first_hbm, first, sems.at[steps + 2]),
        pltpu.make_async_copy(second_hbm, second, sems.at[steps + 3]),
    ]
    for copy in small + tiles + states:
        copy.start()
    core = this_core()
    at = lax.broadcasted_iota(jnp.int32, (rows, rows), 0)
    column = lax.broadcasted_iota(jnp.int32, (rows, rows), 1)
    source = at
    for copy in small:
        copy.wait()
    for place in range(replicas):
        at_place, mine = place_of_row(place % (replicas // 2)), place // (replicas // 2)
        lane = core if mine else 1 - core
        owner = owner_at(at_place, replicas // 2, lane, SUM_MOVES, False)
        inside = (at >= place * block) & (at < (place + 1) * block)
        source = jnp.where(inside, at + (order[owner] - place) * block, source)
    chosen = jnp.where(column == source, 1.0, 0.0).astype(acts.dtype)
    both = jnp.dot(chosen, acts[...], preferred_element_type=jnp.float32).astype(picked.dtype)
    picked[...] = both[half:]
    line = lax.broadcasted_iota(jnp.int32, table.shape, 0)
    value = jnp.zeros(table.shape, jnp.int32)
    for place in range(replicas):
        at_place, far = place % (replicas // 2), place // (replicas // 2)
        owner = owner_at(at_place, replicas // 2, 1 - core if far else core, GATHER_MOVES, True)
        value = jnp.where(line == place, order[owner] * block, value)
    table[...] = value
    mine = both[:half]
    for copy, span in zip(tiles, spans):
        copy.wait()
        product = jnp.dot(mine, grads[:, span], preferred_element_type=jnp.float32)
        product = (product * (1.0 / tokens)).astype(first_send.dtype)
        first_send[:, span] = product[:block]
        other_send[:, span] = product[block:]
    for at, (copy, state) in enumerate(zip(states, (first, second))):
        copy.wait()
        moments[at * block : (at + 1) * block] = state[...].astype(moments.dtype)


def slab_to_send(order, acts_t, grads_out, first, second, steps):
    rows, tokens = acts_t.shape
    block = first.shape[0]
    width = grads_out.shape[1]
    return pl.pallas_call(
        send_kernel,
        in_specs=[HBM()] * 5,
        out_specs=[VMEM()] * 8,
        out_shape=[
            jax.ShapeDtypeStruct((block, width), jnp.bfloat16),
            jax.ShapeDtypeStruct((rows // 2 - block, width), jnp.bfloat16),
            jax.ShapeDtypeStruct((tokens, width), grads_out.dtype),
            jax.ShapeDtypeStruct((rows // 2, tokens), acts_t.dtype),
            jax.ShapeDtypeStruct((block, width), jnp.float32),
            jax.ShapeDtypeStruct((block, width), jnp.float32),
            jax.ShapeDtypeStruct((2 * block, width), jnp.bfloat16),
            jax.ShapeDtypeStruct((order.shape[0], 128), jnp.int32),
        ],
        scratch_shapes=[
            pltpu.SMEM(order.shape, order.dtype),
            pltpu.VMEM((rows, tokens), acts_t.dtype),
            pltpu.SemaphoreType.DMA((steps + 4,)),
        ],
        compiler_params=params(),
        cost_estimate=cost(rows * tokens * width, 2 * tokens * width),
        name="slab_to_send",
    )(*in_hbm(order, acts_t, grads_out, first, second))


def keep_kernel(picked, grads, keep_ref):
    tokens = grads.shape[0]
    tile = grads.shape[1] // 4
    for step in range(4):
        span = pl.ds(step * tile, tile)
        product = jnp.dot(picked[...], grads[:, span], preferred_element_type=jnp.float32)
        keep_ref[:, span] = product * (1.0 / tokens)


def slab_to_keep(picked, grads):
    rows, tokens = picked.shape
    width = grads.shape[1]
    return pl.pallas_call(
        keep_kernel,
        in_specs=[VMEM()] * 2,
        out_specs=VMEM(),
        out_shape=jax.ShapeDtypeStruct((rows, width), jnp.float32),
        compiler_params=params(),
        cost_estimate=cost(2 * rows * tokens * width, 2 * tokens * width),
        name="slab_to_keep",
    )(picked, grads)


def back_kernel(scale, core, weights_hbm, grads, *refs):
    out, weights, result, sems, sem = refs[-5:]
    steps = sems.shape[0]
    tile = grads.shape[1] // steps

    @pl.when(this_core() == core)
    def _():
        spans = [pl.ds(step * tile, tile) for step in range(steps)]
        copies = [
            pltpu.make_async_copy(weights_hbm.at[:, span], weights.at[:, span], sems.at[step])
            for step, span in enumerate(spans)
        ]
        for copy in copies:
            copy.start()
        total = None
        for copy, span in zip(copies, spans):
            copy.wait()
            term = lax.dot_general(
                weights[:, span], grads[:, span], (((1,), (1,)), ((), ())),
                preferred_element_type=jnp.float32,
            )
            total = term if total is None else total + term
        result[...] = (total * scale).astype(result.dtype)
        copy = pltpu.make_async_copy(result, out, sem)
        copy.start()
        copy.wait()


def hidden_gradient(weights_old, grads, core, steps, earlier=()):
    rows, width = weights_old.shape
    tokens = grads.shape[0]
    return pl.pallas_call(
        functools.partial(back_kernel, width ** (-0.5), core),
        in_specs=[HBM(), VMEM()] + [HBM()] * len(earlier),
        out_specs=HBM(),
        out_shape=jax.ShapeDtypeStruct((rows, tokens), jnp.bfloat16),
        input_output_aliases={2 + at: at for at in range(len(earlier))},
        scratch_shapes=[
            pltpu.VMEM((rows, width), weights_old.dtype),
            pltpu.VMEM((rows, tokens), jnp.bfloat16),
            pltpu.SemaphoreType.DMA((steps,)),
            pltpu.SemaphoreType.DMA,
        ],
        compiler_params=params(),
        cost_estimate=cost(2 * rows * tokens * width, 2 * (tokens + rows) * width),
        name="hidden_gradient",
    )(*in_hbm(weights_old), grads, *earlier)


def pair_kernel(start, keep_ref, got_ref, *out_refs):
    block = out_refs[0].shape[0]
    for at, out in enumerate(out_refs):
        kept = keep_ref[(start + at) * block : (start + at + 1) * block]
        got = got_ref[at * block : (at + 1) * block].astype(jnp.float32)
        out[...] = (kept + got).astype(out.dtype)


def pair_sum(keep, got, start, types):
    width = keep.shape[1]
    block = got.shape[0] // len(types)
    return pl.pallas_call(
        functools.partial(pair_kernel, start),
        in_specs=[VMEM(), VMEM()],
        out_specs=[VMEM()] * len(types),
        out_shape=[jax.ShapeDtypeStruct((block, width), kind) for kind in types],
        compiler_params=params(),
        cost_estimate=cost(got.size, 8 * got.size),
        name="pair_sum",
    )(keep, got)


def rates_kernel(count, master_hbm, out, master, sem):
    copy = pltpu.make_async_copy(master_hbm, master, sem)
    copy.start()
    line = lax.broadcasted_iota(jnp.int32, out.shape, 0)
    log = jnp.where(line < out.shape[0] // 2, math.log(0.9), math.log(0.95))
    out[...] = 1.0 - jnp.exp(count[0].astype(jnp.float32) * log)
    copy.wait()


def corrections(count, master):
    return pl.pallas_call(
        rates_kernel,
        in_specs=[SMEM(), HBM()],
        out_specs=[VMEM()] * 2,
        out_shape=[
            jax.ShapeDtypeStruct((16, 128), jnp.float32),
            jax.ShapeDtypeStruct(master.shape, master.dtype),
        ],
        scratch_shapes=[pltpu.SemaphoreType.DMA],
        compiler_params=params(),
        cost_estimate=cost(0, 8 * master.size),
        name="corrections",
    )(count, *in_hbm(master))


def update_kernel(fix, *refs):
    parts, (master, first, second, grads_ref, send_master, send_grads) = refs[:-6], refs[-6:]
    grads = parts[0][...]
    for part in parts[1:]:
        grads = grads + part[...].astype(jnp.float32)
    grads_ref[...] = grads
    send_grads[...] = grads.astype(send_grads.dtype)
    new_master, _, _ = adam_update(
        grads, master[...], first[...], second[...], fix[0:1, 0:1], fix[8:9, 0:1]
    )
    send_master[...] = new_master.astype(send_master.dtype)


def update(fix, parts, states):
    block, width = parts[0].shape
    return pl.pallas_call(
        update_kernel,
        in_specs=[VMEM()] * (4 + len(parts)),
        out_specs=[VMEM()] * 3,
        out_shape=[
            jax.ShapeDtypeStruct((block, width), jnp.float32),
            jax.ShapeDtypeStruct((block, width), jnp.bfloat16),
            jax.ShapeDtypeStruct((block, width), jnp.bfloat16),
        ],
        compiler_params=params(),
        cost_estimate=cost(20 * block * width, 24 * block * width),
        name="update",
    )(fix, *parts, *states)


def states_kernel(fix, master, first, second, grads, *outs):
    updated = adam_update(
        grads[...], master[...], first[...], second[...], fix[0:1, 0:1], fix[8:9, 0:1]
    )
    for out, value in zip(outs, updated):
        out[...] = value


def new_states(fix, states, grads):
    shape = states[0].shape
    return pl.pallas_call(
        states_kernel,
        in_specs=[VMEM()] * 5,
        out_specs=[VMEM()] * 3,
        out_shape=[jax.ShapeDtypeStruct(shape, jnp.float32)] * 3,
        compiler_params=params(),
        cost_estimate=cost(20 * states[0].size, 28 * states[0].size),
        name="new_states",
    )(fix, *states, grads)


def placing(places, chips, table, near, far, weights, sems):
    block = near[0].shape[0]
    rows = table[...]
    copies = []
    for at, *pieces in zip(places, near, far):
        for sibling, piece in enumerate(pieces):
            row = pl.multiple_of(rows[at + sibling * chips, 0], block)
            target = weights.at[pl.ds(row, block), :]
            copies.append(pltpu.make_async_copy(piece, target, sems.at[len(copies)]))
    return copies


def early_kernel(chips, table, *refs):
    count = chips - 1
    copies = placing(range(count), chips, table, refs[:count], refs[count : 2 * count], *refs[-2:])
    for copy in copies:
        copy.start()
    for copy in copies:
        copy.wait()


def place_early(table, near, far):
    block, width = near[0].shape
    chips = len(near) + 1
    return pl.pallas_call(
        functools.partial(early_kernel, chips),
        in_specs=[VMEM()] * (2 * chips - 1),
        out_specs=HBM(),
        out_shape=jax.ShapeDtypeStruct((2 * chips * block, width), jnp.bfloat16),
        scratch_shapes=[pltpu.SemaphoreType.DMA((2 * chips - 2,))],
        compiler_params=params(),
        cost_estimate=cost(0, 8 * chips * block * width),
        name="place_early",
    )(table, *near, *far)


def late_kernel(chips, table, near, *refs):
    far, (packed, moved, _, weights, checkpoint, partner, sems) = refs[:chips], refs[chips:]
    block = moved.shape[0]
    replicas = 2 * chips
    me = lax.axis_index("replica")
    previous = lax.rem(me + replicas - 1, replicas)
    copies = placing([chips - 1], chips, table, [near], far[-1:], weights, sems)
    for copy in copies:
        copy.start()
    grads = moved[...].astype(jnp.float32)
    partner[1] = 0.9 * packed[:block].astype(jnp.float32) + 0.1 * grads
    partner[2] = 0.95 * packed[block:].astype(jnp.float32) + 0.05 * grads * grads
    for at, piece in enumerate(far):

        @pl.when(owner_at(at, chips, 1 - me % 2, GATHER_MOVES, True) == previous)
        def _():
            partner[0] = piece[...].astype(jnp.float32)

    last = pltpu.make_async_copy(partner, checkpoint, sems.at[2])
    last.start()
    for copy in copies:
        copy.wait()
    last.wait()


def place_late(table, near, far, packed, moved, weights):
    block, width = moved.shape
    chips = len(far)
    return pl.pallas_call(
        functools.partial(late_kernel, chips),
        in_specs=[VMEM()] * (chips + 4) + [HBM()],
        out_specs=[HBM()] * 2,
        out_shape=[
            jax.ShapeDtypeStruct(weights.shape, weights.dtype),
            jax.ShapeDtypeStruct((3, block, width), jnp.float32),
        ],
        input_output_aliases={chips + 4: 0},
        scratch_shapes=[
            pltpu.VMEM((3, block, width), jnp.float32),
            pltpu.SemaphoreType.DMA((3,)),
        ],
        compiler_params=params(),
        cost_estimate=cost(0, 20 * block * width),
        name="place_late",
    )(table, near, *far, packed, moved, weights)


def tiled_device(
    hidden, out_grad, weights_old, master, first_moment, second_moment, owner_order, step_count
):
    replicas = lax.axis_size("replica")
    chips = replicas // 2

    def permuted(piece, target):
        return lax.ppermute(piece, "replica", [(i, target(i)) for i in range(replicas)])

    def across(piece, at, moves):
        def target(i):
            return 2 * moved_chip(i // 2, chips, move_of(moves, chips, i % 2, at)) + i % 2

        return permuted(piece, target)

    def to_sibling(piece):
        return permuted(piece, lambda i: i ^ 1)

    def along_ring(piece):
        return permuted(piece, lambda i: (i + 1) % replicas)

    send_first, send_other, grads_out, picked, first, second, packed, table = slab_to_send(
        owner_order, hidden[0].T, out_grad[0], first_moment, second_moment, 4
    )
    got_first = to_sibling(send_first)
    got_other = to_sibling(send_other)
    keep = slab_to_keep(picked, grads_out)
    packed = along_ring(packed)
    sends = pair_sum(keep, got_first, 0, [jnp.bfloat16])
    own, *others = pair_sum(
        keep, got_other, 1, [jnp.float32] + [jnp.bfloat16] * (chips - 2)
    )
    sends = [*sends, *others]
    hidden_grad = hidden_gradient(weights_old, grads_out, 1, 1)
    hidden_grad = hidden_gradient(weights_old, grads_out, 0, 1, (hidden_grad,))
    parts = [own] + [across(sends[k - 1], k, SUM_MOVES) for k in range(1, chips)]
    fix, loaded = corrections(lax.optimization_barrier((step_count, own))[0], master)
    states = (loaded, first, second)
    grads, send_master, send_grads = update(fix, parts, states)
    near = [send_master] + [across(send_master, k, GATHER_MOVES) for k in range(1, chips)]
    updated = new_states(fix, states, grads)
    moved = along_ring(send_grads)
    far = [to_sibling(piece) for piece in near]
    weights_new = place_early(table, near[:-1], far[:-1])
    weights_new, checkpoint = place_late(table, near[-1], far, packed, moved, weights_new)
    return (*updated, checkpoint, weights_new, hidden_grad.T[None])


def fits(replicas, block, width):
    chips = replicas // 2
    return block % 8 == 0 and width % 512 == 0 and replicas % 2 == 0 and chips & (chips - 1) == 0


def per_device(*arrays):
    block, width = arrays[3].shape
    if not fits(lax.axis_size("replica"), block, width):
        return plain_device(*arrays)
    return tiled_device(*arrays)


def solution(mesh):
    devices = P(("section", "replica"), None)
    return jax.shard_map(
        per_device,
        mesh=mesh,
        in_specs=(
            P("section", "replica", None),
            P("section", "replica", None),
            P("section", None),
            devices,
            devices,
            devices,
            P(),
            P(),
        ),
        out_specs=(
            devices,
            devices,
            devices,
            P(None, ("section", "replica"), None),
            P("section", None),
            P("section", "replica", None),
        ),
        check_vma=False,
    )
```
